32 devices in a mesh: dp: 8 (over y, x, core), tensor: 4 (over z).
Axes of the slice: x: 2, y: 2, z: 4, core: 2. Of those that a mesh axis runs over, the one named last changes fastest.
Arguments:
- block_in: float32 [8192, 2048], P(('dp', 'tensor')), may hold values from -6 to 6
- out_grad: float32 [8192, 2048], P(('dp', 'tensor')), may hold values from -6 to 6
- segment_ids: int32 [8, 1024], P('dp'), may hold values from -1 to 6, as said below
- w_query: bfloat16 [2048, 2048], P(None, 'tensor'), may hold values from -8 to 8
- w_key: bfloat16 [2048, 512], P(None, 'tensor'), may hold values from -0.125 to 0.125
- w_value: bfloat16 [2048, 512], P(None, 'tensor'), may hold values from -0.125 to 0.125
- w_out: bfloat16 [2048, 2048], P('tensor'), may hold values from -1 to 1
- w_gate: bfloat16 [2048, 8192], P(None, 'tensor'), may hold values from -0.125 to 0.125
- w_up: bfloat16 [2048, 8192], P(None, 'tensor'), may hold values from -0.125 to 0.125
- w_down: bfloat16 [8192, 2048], P('tensor'), may hold values from -0.0625 to 0.0625
- gain_attn: float32 [2048], replicated, may hold values from 0.5 to 1.5
- gain_mlp: float32 [2048], replicated, may hold values from 0.5 to 1.5
Outputs:
- block_out: float32 [8192, 2048], P(('dp', 'tensor'))
- input_grad: float32 [8192, 2048], P(('dp', 'tensor'))
- grad_w_query: float32 [2048, 2048], P('dp', 'tensor')
- grad_w_key: float32 [2048, 512], P('dp', 'tensor')
- grad_w_value: float32 [2048, 512], P('dp', 'tensor')
- grad_w_out: float32 [2048, 2048], P('tensor', 'dp')
- grad_w_gate: float32 [2048, 8192], P('dp', 'tensor')
- grad_w_up: float32 [2048, 8192], P('dp', 'tensor')
- grad_w_down: float32 [8192, 2048], P('tensor', 'dp')
- grad_gain_attn: float32 [2048], P('dp')
- grad_gain_mlp: float32 [2048], P('dp')
The draws below stay inside these ranges and needn't reach their ends.
Inputs may be any that keep to these rules, and one draw needn't show every extreme that they name: In each row of segment_ids the ids of the live tokens never fall, padding (-1) only follows the live tokens, each sequence is a run of at most 512 tokens, and in every draw some row has no padding and a sequence of exactly 512 tokens.
All inputs are finite; a program needn't handle non-finite values.
Results may differ from the reference program's by a relative error of at most 0.023.
Values may be sent and summed in bfloat16 or wider, within the bound.
No kernel may reach another device: no remote copies, remote signals or barrier semaphores. Data moves between devices by JAX's collectives and lax.ppermute only.
A program may use at most 256 MiB of HBM per device.

```python
import math
import jax
import jax.numpy as jnp
from jax import lax

D = 2048
HEADS = 32
KV_HEADS = 8
HEAD_DIM = 64
FF = 8192
TOK_DEV = 1024
MAXLEN = 512
BATCHES = 8
TOKENS = 8192


def draw_w_query(key, part):
    values = jax.random.normal(key, (D, HEADS * HEAD_DIM), jnp.float32) * D ** (-0.5)
    return values.astype(jnp.bfloat16)


def draw_segment_ids(key, part):
    full_row = jax.random.randint(jax.random.fold_in(key, 1), (), 0, BATCHES)
    is_full = jnp.arange(BATCHES, dtype=jnp.int32) == full_row
    most_row = (full_row + 1) % BATCHES
    is_most = jnp.arange(BATCHES, dtype=jnp.int32) == most_row
    live_count = jax.random.randint(jax.random.fold_in(key, 2), (BATCHES,), TOK_DEV // 4, TOK_DEV + 1)
    live_count = jnp.where(is_full | is_most, TOK_DEV, live_count)
    offset = jax.random.randint(jax.random.fold_in(key, 3), (BATCHES,), 0, MAXLEN)
    offset = jnp.where(is_most, 0, offset)
    extra_count = 2 * (TOK_DEV // MAXLEN)
    cut_points = jax.random.randint(jax.random.fold_in(key, 4), (BATCHES, extra_count), 1, TOK_DEV)
    cut_points = jnp.where(is_full[:, None], TOK_DEV, cut_points)
    position = jnp.arange(TOK_DEV, dtype=jnp.int32)[None, :]
    shifted = position - offset[:, None]
    forced = jnp.where(shifted >= 0, jnp.maximum(shifted, 0) // MAXLEN + 1, 0)
    extra_cuts = jnp.sum((cut_points[:, None, :] <= position[:, :, None]).astype(jnp.int32), axis=-1)
    seq_ids = forced + extra_cuts
    return jnp.where(position < live_count[:, None], seq_ids, -1).astype(jnp.int32)


def steps_of(stream_key, shape, pieces, smallest, top_value):
    def one(dim, shards_of):
        draws = jax.random.uniform(jax.random.fold_in(jax.random.fold_in(stream_key, 6), dim), (shards_of,), jnp.float32, smallest / len(pieces), top_value / len(pieces))
        return jnp.repeat(jnp.exp(draws), shape[dim] // shards_of).reshape((-1,) + (1,) * (len(shape) - dim - 1))

    gain = one(*pieces[0])
    for cut in pieces[1:]:
        gain = gain * one(*cut)
    return gain


def bell_draw(rng, dims, scale, bound, shards=(), kind=jnp.bfloat16):
    level = steps_of(rng, dims, shards, -0.22, 0.18) if shards else 1.0
    values = jax.random.normal(rng, dims, jnp.float32) * scale * level
    return jnp.minimum(jnp.maximum(values, -bound), bound).astype(kind)


def setup_inputs(seed: int = 0) -> dict:
    key_of = jax.random.split(jax.random.key(seed), 13)
    return {
        "block_in": bell_draw(key_of[0], (TOKENS, D), 1.0, 6.0, ((0, 32),), jnp.float32),
        "out_grad": bell_draw(key_of[1], (TOKENS, D), 1.0, 6.0, ((0, 32),), jnp.float32),
        "segment_ids": draw_segment_ids(jax.random.fold_in(key_of[12], 71), 0),
        "w_query": draw_w_query(jax.random.fold_in(key_of[12], 71), 0),
        "w_key": bell_draw(key_of[4], (D, KV_HEADS * HEAD_DIM), D ** -0.5, 0.125, ((1, 4),)),
        "w_value": bell_draw(key_of[5], (D, KV_HEADS * HEAD_DIM), D ** -0.5, 0.125, ((1, 4),)),
        "w_out": bell_draw(key_of[6], (HEADS * HEAD_DIM, D), (HEADS * HEAD_DIM // 64) ** -0.5, 1.0, ((0, 4),)),
        "w_gate": bell_draw(key_of[7], (D, FF), D ** -0.5, 0.125, ((1, 4),)),
        "w_up": bell_draw(key_of[8], (D, FF), D ** -0.5, 0.125, ((1, 4),)),
        "w_down": bell_draw(key_of[9], (FF, D), FF ** -0.5, 0.0625, ((0, 4),)),
        "gain_attn": jnp.clip(1.0 + 0.1 * jax.random.normal(key_of[10], (D,), jnp.float32), 0.5, 1.5),
        "gain_mlp": jnp.clip(1.0 + 0.1 * jax.random.normal(key_of[11], (D,), jnp.float32), 0.5, 1.5),
    }


epsilon = 1e-05

def rope_tables(positions):
    half_dim = HEAD_DIM // 2
    index_vals = jnp.arange(half_dim, dtype=jnp.float32)
    base_freq = jnp.exp(-(2.0 * index_vals / HEAD_DIM) * math.log(500000.0))
    wavelen = 2.0 * math.pi / base_freq
    smooth = (8192.0 / wavelen - 1.0) / 3.0
    middle_freq = (1.0 - smooth) * base_freq / 32.0 + smooth * base_freq
    scaled = jnp.where(wavelen > 8192.0, base_freq / 32.0, jnp.where(wavelen < 2048.0, base_freq, middle_freq))
    angles = positions.astype(jnp.float32)[:, None] * scaled[None, :]
    return (jnp.cos(angles), jnp.sin(angles))

def rotate_heads(values, cosines, sine_table, direction):
    half_dim = HEAD_DIM // 2
    front_half = values[..., :half_dim]
    back_half = values[..., half_dim:]
    cos_part = cosines[:, None, :]
    sin_part = sine_table[:, None, :] * direction
    return jnp.concatenate([front_half * cos_part - back_half * sin_part, back_half * cos_part + front_half * sin_part], axis=-1)

def run_positions(seq_row):
    count_rows = seq_row.shape[0]
    index_vals = jnp.arange(count_rows, dtype=jnp.int32)
    change = jnp.concatenate([jnp.ones((1,), dtype=bool), seq_row[1:] != seq_row[:-1]])
    run_start = lax.cummax(jnp.where(change, index_vals, jnp.zeros_like(index_vals)), axis=0)
    return index_vals - run_start

def allowed_pairs(number, seq_row, padded_ids, span_rows):
    query_idx = number * span_rows + jnp.arange(span_rows, dtype=jnp.int32)
    key_idx = (number - 1) * span_rows + jnp.arange(2 * span_rows, dtype=jnp.int32)
    query_ids = lax.dynamic_slice_in_dim(seq_row, number * span_rows, span_rows)
    key_ids = lax.dynamic_slice_in_dim(padded_ids, number * span_rows, 2 * span_rows)
    same_seq = (query_ids[:, None] == key_ids[None, :]) & (query_ids[:, None] >= 0) & (key_idx[None, :] <= query_idx[:, None])
    return same_seq | (key_idx[None, :] == query_idx[:, None])

def padded_inputs(key_rows, value_rows, seq_row, span_rows):
    zero_rows = jnp.zeros((span_rows, key_rows.shape[1]), jnp.bfloat16)
    key_pad = jnp.concatenate([zero_rows, key_rows], axis=0)
    value_pad = jnp.concatenate([zero_rows, value_rows], axis=0)
    padded_ids = jnp.concatenate([jnp.full((span_rows,), -2, jnp.int32), seq_row.astype(jnp.int32)])
    return (key_pad, value_pad, padded_ids)

def block_scores(queries, key_pad, seq_row, padded_ids, number, span_rows, head_count, group_count):
    group_size = head_count // group_count
    query_blk = lax.dynamic_slice_in_dim(queries, number * span_rows, span_rows).reshape(span_rows, group_count, group_size, HEAD_DIM)
    key_blk = lax.dynamic_slice_in_dim(key_pad, number * span_rows, 2 * span_rows).reshape(2 * span_rows, group_count, HEAD_DIM)
    scores = jnp.einsum('agrd,bgd->grab', query_blk.astype(jnp.float32), key_blk.astype(jnp.float32)) * HEAD_DIM ** (-0.5)
    allowed = allowed_pairs(number, seq_row, padded_ids, span_rows)
    return (jnp.where(allowed[None, None], scores, -1e+30), query_blk, key_blk)

def attention_forward(queries, key_rows, value_rows, seq_row, span_rows):
    total_rows = queries.shape[0]
    head_count = queries.shape[1] // HEAD_DIM
    group_count = key_rows.shape[1] // HEAD_DIM
    group_size = head_count // group_count
    key_pad, value_pad, padded_ids = padded_inputs(key_rows, value_rows, seq_row, span_rows)

    def attend_block(number):
        scores, query_blk, key_blk = block_scores(queries, key_pad, seq_row, padded_ids, number, span_rows, head_count, group_count)
        value_blk = lax.dynamic_slice_in_dim(value_pad, number * span_rows, 2 * span_rows).reshape(2 * span_rows, group_count, HEAD_DIM)
        row_max = lax.optimization_barrier(jnp.max(scores, axis=-1, keepdims=True))
        log_total = row_max + jnp.log(lax.optimization_barrier(jnp.sum(jnp.exp(scores - row_max), axis=-1, keepdims=True)))
        attn_probs = jnp.exp(scores - log_total).astype(jnp.bfloat16)
        result = jnp.einsum('grab,bgd->agrd', attn_probs.astype(jnp.float32), value_blk.astype(jnp.float32))
        return (result.reshape(span_rows, head_count * HEAD_DIM).astype(jnp.bfloat16), log_total[..., 0])
    count_blocks = total_rows // span_rows
    results, log_totals = lax.map(attend_block, jnp.arange(count_blocks, dtype=jnp.int32))
    return (results.reshape(total_rows, head_count * HEAD_DIM), log_totals)

def attention_backward(queries, key_rows, value_rows, attended, d_attended, log_totals, seq_row, span_rows):
    total_rows = queries.shape[0]
    head_count = queries.shape[1] // HEAD_DIM
    group_count = key_rows.shape[1] // HEAD_DIM
    group_size = head_count // group_count
    key_pad, value_pad, padded_ids = padded_inputs(key_rows, value_rows, seq_row, span_rows)

    def back_block(carry, number):
        key_grads, value_grads = carry
        scores, query_blk, key_blk = block_scores(queries, key_pad, seq_row, padded_ids, number, span_rows, head_count, group_count)
        value_blk = lax.dynamic_slice_in_dim(value_pad, number * span_rows, 2 * span_rows).reshape(2 * span_rows, group_count, HEAD_DIM)
        log_total = lax.dynamic_index_in_dim(log_totals, number, 0, keepdims=False)
        prob_full = jnp.exp(scores - log_total[..., None])
        attn_probs = prob_full.astype(jnp.bfloat16)
        grad_blk = lax.dynamic_slice_in_dim(d_attended, number * span_rows, span_rows)
        out_blk = lax.dynamic_slice_in_dim(attended, number * span_rows, span_rows)
        row_delta = lax.optimization_barrier(jnp.sum((grad_blk.astype(jnp.float32) * out_blk.astype(jnp.float32)).reshape(span_rows, head_count, HEAD_DIM), axis=-1))
        row_delta = jnp.transpose(row_delta.reshape(span_rows, group_count, group_size), (1, 2, 0))
        grad_heads = grad_blk.reshape(span_rows, group_count, group_size, HEAD_DIM).astype(jnp.float32)
        d_probs = jnp.einsum('agrd,bgd->grab', grad_heads, value_blk.astype(jnp.float32))
        d_scores = (prob_full * (d_probs - row_delta[..., None])).astype(jnp.bfloat16).astype(jnp.float32)
        d_query_blk = jnp.einsum('grab,bgd->agrd', d_scores, key_blk.astype(jnp.float32)) * HEAD_DIM ** (-0.5)
        d_key_blk = jnp.einsum('grab,agrd->bgd', d_scores, query_blk.astype(jnp.float32)) * HEAD_DIM ** (-0.5)
        d_value_blk = jnp.einsum('grab,agrd->bgd', attn_probs.astype(jnp.float32), grad_heads)
        old_keys = lax.dynamic_slice_in_dim(key_grads, number * span_rows, 2 * span_rows)
        old_values = lax.dynamic_slice_in_dim(value_grads, number * span_rows, 2 * span_rows)
        key_grads = lax.dynamic_update_slice_in_dim(key_grads, old_keys + d_key_blk, number * span_rows, 0)
        value_grads = lax.dynamic_update_slice_in_dim(value_grads, old_values + d_value_blk, number * span_rows, 0)
        return ((key_grads, value_grads), d_query_blk.reshape(span_rows, head_count, HEAD_DIM))
    start_grads = jnp.zeros((total_rows + span_rows, group_count, HEAD_DIM), jnp.float32)
    count_blocks = total_rows // span_rows
    (key_grads, value_grads), d_queries = lax.scan(back_block, (start_grads, start_grads), jnp.arange(count_blocks, dtype=jnp.int32))
    return (d_queries.reshape(total_rows, head_count, HEAD_DIM), key_grads[span_rows:], value_grads[span_rows:])

def inner_rows(left, right):
    return lax.dot_general(left, right, (((0,), (0,)), ((), ())), preferred_element_type=jnp.float32)

def outer_cols(left, weight_mat):
    return lax.dot_general(left, weight_mat, (((1,), (1,)), ((), ())), preferred_element_type=jnp.float32)

def layer(block_in, out_grad, seq_row, w_query, w_key, w_value, w_out, w_gate, w_up, w_down, gain_attn, gain_mlp):
    total_rows = block_in.shape[0]
    head_count = w_query.shape[1] // HEAD_DIM
    group_count = w_key.shape[1] // HEAD_DIM
    positions = run_positions(seq_row)
    cosines, sine_table = rope_tables(positions)
    live_rows = (seq_row >= 0).astype(jnp.float32)
    inv_one = lax.rsqrt(lax.optimization_barrier(jnp.mean(block_in * block_in, axis=1, keepdims=True)) + epsilon)
    normed_one = block_in * inv_one
    attn_in = (normed_one * gain_attn).astype(jnp.bfloat16)
    query_pre = jnp.dot(attn_in, w_query, preferred_element_type=jnp.float32)
    key_pre = jnp.dot(attn_in, w_key, preferred_element_type=jnp.float32)
    value_rows = jnp.dot(attn_in, w_value, preferred_element_type=jnp.float32).astype(jnp.bfloat16)
    queries = rotate_heads(query_pre.reshape(total_rows, head_count, HEAD_DIM), cosines, sine_table, 1.0).reshape(total_rows, -1).astype(jnp.bfloat16)
    key_rows = rotate_heads(key_pre.reshape(total_rows, group_count, HEAD_DIM), cosines, sine_table, 1.0).reshape(total_rows, -1).astype(jnp.bfloat16)
    attended, log_totals = attention_forward(queries, key_rows, value_rows, seq_row, MAXLEN)
    middle = block_in + jnp.dot(attended, w_out, preferred_element_type=jnp.float32)
    inv_two = lax.rsqrt(lax.optimization_barrier(jnp.mean(middle * middle, axis=1, keepdims=True)) + epsilon)
    normed_two = middle * inv_two
    mlp_in = (normed_two * gain_mlp).astype(jnp.bfloat16)
    gate_pre = jnp.dot(mlp_in, w_gate, preferred_element_type=jnp.float32)
    up_proj = jnp.dot(mlp_in, w_up, preferred_element_type=jnp.float32)
    sigmoid_vals = jax.nn.sigmoid(gate_pre)
    gate_act = gate_pre * sigmoid_vals
    hidden = (gate_act * up_proj).astype(jnp.bfloat16)
    block_out = middle + jnp.dot(hidden, w_down, preferred_element_type=jnp.float32)
    masked_grad = out_grad * live_rows[:, None]
    grad_rows = masked_grad.astype(jnp.bfloat16)
    grad_down = inner_rows(hidden, grad_rows)
    d_hidden = outer_cols(grad_rows, w_down)
    d_gate = (d_hidden * up_proj * sigmoid_vals * (1.0 + gate_pre * (1.0 - sigmoid_vals))).astype(jnp.bfloat16)
    d_up = (d_hidden * gate_act).astype(jnp.bfloat16)
    grad_gate = inner_rows(mlp_in, d_gate)
    grad_up = inner_rows(mlp_in, d_up)
    d_mlp_in = outer_cols(d_gate, w_gate) + outer_cols(d_up, w_up)
    grad_gain_mlp = lax.optimization_barrier(jnp.sum(d_mlp_in * normed_two, axis=0))
    d_normed_two = d_mlp_in * gain_mlp
    d_middle = masked_grad + inv_two * (d_normed_two - normed_two * lax.optimization_barrier(jnp.mean(d_normed_two * normed_two, axis=1, keepdims=True)))
    mid_rows = d_middle.astype(jnp.bfloat16)
    grad_out = inner_rows(attended, mid_rows)
    d_attended = outer_cols(mid_rows, w_out).astype(jnp.bfloat16)
    d_queries, d_keys, d_values = attention_backward(queries, key_rows, value_rows, attended, d_attended, log_totals, seq_row, MAXLEN)
    d_q_rows = rotate_heads(d_queries, cosines, sine_table, -1.0).reshape(total_rows, -1).astype(jnp.bfloat16)
    d_k_rows = rotate_heads(d_keys, cosines, sine_table, -1.0).reshape(total_rows, -1).astype(jnp.bfloat16)
    d_v_rows = d_values.reshape(total_rows, -1).astype(jnp.bfloat16)
    grad_query = inner_rows(attn_in, d_q_rows)
    grad_key = inner_rows(attn_in, d_k_rows)
    grad_value = inner_rows(attn_in, d_v_rows)
    d_attn_in = outer_cols(d_q_rows, w_query) + outer_cols(d_k_rows, w_key) + outer_cols(d_v_rows, w_value)
    grad_gain_attn = lax.optimization_barrier(jnp.sum(d_attn_in * normed_one, axis=0))
    d_normed_one = d_attn_in * gain_attn
    input_grad = d_middle + inv_one * (d_normed_one - normed_one * lax.optimization_barrier(jnp.mean(d_normed_one * normed_one, axis=1, keepdims=True)))
    grads = (grad_query, grad_key, grad_value, grad_out, grad_gate, grad_up, grad_down, grad_gain_attn, grad_gain_mlp)
    return (block_out, input_grad, grads)

def reference(block_in, out_grad, segment_ids, w_query, w_key, w_value, w_out, w_gate, w_up, w_down, gain_attn, gain_mlp):
    inputs = (block_in.reshape(BATCHES, TOK_DEV, D), out_grad.reshape(BATCHES, TOK_DEV, D), segment_ids)
    shapes = (w_query.shape, w_key.shape, w_value.shape, w_out.shape, w_gate.shape, w_up.shape, w_down.shape, gain_attn.shape, gain_mlp.shape)
    start_totals = tuple((jnp.zeros(shape_item, jnp.float32) for shape_item in shapes))

    def accumulate(totals, batch_inputs):
        out_rows, grad_in_rows, grads = layer(batch_inputs[0], batch_inputs[1], batch_inputs[2], w_query, w_key, w_value, w_out, w_gate, w_up, w_down, gain_attn, gain_mlp)
        return (tuple((total + grad for total, grad in zip(totals, grads))), (out_rows, grad_in_rows))
    totals, (out_rows, grad_in_rows) = lax.scan(accumulate, start_totals, inputs)
    return (out_rows.reshape(TOKENS, D), grad_in_rows.reshape(TOKENS, D), totals[0], totals[1], totals[2], totals[3], totals[4], totals[5], totals[6], totals[7], totals[8])
```

```python
import functools
import math

import jax
import jax.numpy as jnp
from jax import lax
from jax.experimental import pallas as pl
from jax.experimental.pallas import tpu as pltpu
from jax.sharding import PartitionSpec as P

HEAD_DIM = 64
MAXLEN = 512
LANES = 128
epsilon = 1e-05
BF = jnp.bfloat16
F32 = jnp.float32
NEG = -1e30
VMEM_CAP = 60 * 1024 * 1024


def rope_tables(positions):
    half_dim = HEAD_DIM // 2
    index_vals = jnp.arange(half_dim, dtype=F32)
    base_freq = jnp.exp(-(2.0 * index_vals / HEAD_DIM) * math.log(500000.0))
    wavelen = 2.0 * math.pi / base_freq
    smooth = (8192.0 / wavelen - 1.0) / 3.0
    middle_freq = (1.0 - smooth) * base_freq / 32.0 + smooth * base_freq
    scaled = jnp.where(
        wavelen > 8192.0, base_freq / 32.0, jnp.where(wavelen < 2048.0, base_freq, middle_freq)
    )
    angles = positions.astype(F32)[:, None] * scaled[None, :]
    cosines, sines = jnp.cos(angles), jnp.sin(angles)
    return (
        jnp.concatenate([cosines] * 4, axis=1),
        jnp.concatenate([-sines, sines, -sines, sines], axis=1),
    )


def run_starts(seq_row):
    index_vals = jnp.arange(seq_row.shape[0], dtype=jnp.int32)
    change = jnp.concatenate([jnp.ones((1,), dtype=bool), seq_row[1:] != seq_row[:-1]])
    return lax.cummax(jnp.where(change, index_vals, jnp.zeros_like(index_vals)), axis=0)


def ring_blocks(array, n, z):
    rows = array.shape[0] // n
    blocks = [array[k * rows : (k + 1) * rows] for k in range(n)]
    twice = jnp.concatenate(blocks[::-1] * 2, axis=0)
    return lax.dynamic_slice_in_dim(twice, (n - 1 - z) * rows, n * rows)


def line_gather(block, n, z):
    right, left = [block], [block]
    for s in range(1, n):
        right.append(lax.ppermute(right[-1], "tensor", [(i, i + 1) for i in range(s - 1, n - 1)]))
        left.append(lax.ppermute(left[-1], "tensor", [(i, i - 1) for i in range(1, n - s + 1)]))
    return [block] + [jnp.where(z >= s, right[s], left[n - s]) for s in range(1, n)]


def line_scatter(parts, n):
    right, left = parts[1], parts[n - 1]
    for s in range(1, n):
        right = lax.ppermute(right, "tensor", [(i, i + 1) for i in range(min(s, n - 1))])
        left = lax.ppermute(left, "tensor", [(i, i - 1) for i in range(n - s, n)])
        if s < n - 1:
            right = (parts[s + 1].astype(F32) + right.astype(F32)).astype(BF)
            left = (parts[n - s - 1].astype(F32) + left.astype(F32)).astype(BF)
    return parts[0].astype(F32) + right.astype(F32) + left.astype(F32)


def nn(a, b, **kw):
    return lax.dot_general(a, b, (((1,), (0,)), ((), ())), preferred_element_type=F32, **kw)


def nt(a, b, **kw):
    return lax.dot_general(a, b, (((1,), (1,)), ((), ())), preferred_element_type=F32, **kw)


def tn(a, b):
    return lax.dot_general(a, b, (((0,), (0,)), ((), ())), preferred_element_type=F32)


def rotate_slab(x, cos, sin, direction):
    lane = lax.broadcasted_iota(jnp.int32, x.shape, 1)
    other = jnp.where(lane % HEAD_DIM < HEAD_DIM // 2, pltpu.roll(x, 96, 1), pltpu.roll(x, 32, 1))
    return x * cos + other * (sin * direction)


def project_kernel(rope_slabs, x_ref, w_ref, cos_ref, sin_ref, out_ref):
    cos, sin = cos_ref[...], sin_ref[...]
    full = nn(x_ref[...], w_ref[...])
    for k in range(w_ref.shape[1] // LANES):
        slab = full[:, k * LANES : (k + 1) * LANES]
        if k < rope_slabs:
            slab = rotate_slab(slab, cos, sin, 1.0)
        out_ref[:, k * LANES : (k + 1) * LANES] = slab.astype(BF)


def project(x, w_aug, cos, sin, rope_slabs, block):
    rows, depth = x.shape
    cols = w_aug.shape[1]
    return pl.pallas_call(
        functools.partial(project_kernel, rope_slabs),
        out_shape=jax.ShapeDtypeStruct((rows, cols), BF),
        grid=(rows // block,),
        in_specs=[
            pl.BlockSpec((block, depth), lambda i: (i, 0)),
            pl.BlockSpec((depth, cols), lambda i: (0, 0)),
            pl.BlockSpec((block, LANES), lambda i: (i, 0)),
            pl.BlockSpec((block, LANES), lambda i: (i, 0)),
        ],
        out_specs=pl.BlockSpec((block, cols), lambda i: (i, 0)),
        cost_estimate=pl.CostEstimate(
            flops=2 * rows * depth * cols,
            bytes_accessed=2 * (rows * depth + depth * cols + rows * cols),
            transcendentals=0,
        ),
        compiler_params=pltpu.CompilerParams(vmem_limit_bytes=VMEM_CAP),
        name="project",
    )(x, w_aug, cos, sin)


def block_offset(z, block_no, n, rows):
    return pl.multiple_of(lax.rem(z - block_no + n, n) * rows, rows)


def bias_of(start_row, first_key, first_query, width, rows):
    key = first_key + lax.broadcasted_iota(jnp.int32, (width, rows), 0)
    query = first_query + lax.broadcasted_iota(jnp.int32, (width, rows), 1)
    ok = (key >= start_row) & (key <= query)
    return jnp.where(ok, jnp.zeros((width, rows), F32), jnp.full((width, rows), NEG, F32))


def window(ref, z, b, back, n, rows):
    parts = [ref[pl.ds(block_offset(z, b - k, n, rows), rows), :] for k in range(back, -1, -1)]
    return parts[0] if len(parts) == 1 else jnp.concatenate(parts, axis=0)


def attend_kernel(n, rows, max_back, z_ref, start_ref, q_ref, k_ref, v_ref, out_ref, lse_ref):
    z = z_ref[0]
    b = pl.program_id(1)
    offset = block_offset(z, b, n, rows)
    lane = lax.broadcasted_iota(jnp.int32, (rows, LANES), 1)

    def body(back):
        width = (back + 1) * rows
        keys = window(k_ref, z, b, back, n, rows)
        values = window(v_ref, z, b, back, n, rows)
        start_row = start_ref[0]
        bias = bias_of(start_row, (b - back) * rows, b * rows, width, rows)
        queries = q_ref[pl.ds(offset, rows), :] * jnp.asarray(HEAD_DIM**-0.5, BF)
        outs, lses = [], []
        for h in range(2):
            mine = (lane >= HEAD_DIM) == (h == 1)
            scores = nt(keys, jnp.where(mine, queries, jnp.zeros_like(queries))) + bias
            top = jnp.max(scores, axis=0, keepdims=True)
            probs = jnp.exp(scores - top)
            total = jnp.sum(probs, axis=0, keepdims=True)
            out_t = tn(values, probs.astype(BF)) / total
            outs.append(out_t[h * HEAD_DIM : (h + 1) * HEAD_DIM])
            lses.append(top + jnp.log(total))
        slab = jnp.concatenate(outs, axis=0).T.astype(BF)
        half = rows // 2
        out_ref[0] = slab[:half]
        out_ref[1] = slab[half:]
        lse_ref[0, 0] = jnp.concatenate(lses, axis=0)

    for back in range(max_back + 1):
        wanted = (b == back) if back < max_back else (b >= back)
        pl.when(wanted)(functools.partial(body, back))


def attend(z, starts, qkv, n, rows, pairs, pairs_per_group):
    total = qkv.shape[0]
    groups = pairs // pairs_per_group
    half = rows // 2
    max_back = min(n - 1, -(-(MAXLEN - 1) // rows))
    return pl.pallas_call(
        functools.partial(attend_kernel, n, rows, max_back),
        out_shape=(
            jax.ShapeDtypeStruct((2, n * half, pairs * LANES), BF),
            jax.ShapeDtypeStruct((pairs, n, 2, rows), F32),
        ),
        grid_spec=pltpu.PrefetchScalarGridSpec(
            num_scalar_prefetch=1,
            grid=(pairs, n),
            in_specs=[
                pl.BlockSpec((1, 1, rows), lambda p, b, z: (b, 0, 0)),
                pl.BlockSpec((total, LANES), lambda p, b, z: (0, p)),
                pl.BlockSpec((total, LANES), lambda p, b, z: (0, pairs + p // pairs_per_group)),
                pl.BlockSpec(
                    (total, LANES), lambda p, b, z: (0, pairs + groups + p // pairs_per_group)
                ),
            ],
            out_specs=[
                pl.BlockSpec((2, half, LANES), lambda p, b, z: (0, lax.rem(z[0] - b + n, n), p)),
                pl.BlockSpec((1, 1, 2, rows), lambda p, b, z: (p, b, 0, 0)),
            ],
        ),
        cost_estimate=pl.CostEstimate(
            flops=4 * total * rows * 3 * pairs * LANES,
            bytes_accessed=4 * total * pairs * LANES,
            transcendentals=total * rows * 3 * pairs * 2,
        ),
        compiler_params=pltpu.CompilerParams(vmem_limit_bytes=VMEM_CAP),
        name="attend",
    )(z, starts, qkv, qkv, qkv)


def attend_back_kernel(
    n,
    rows,
    max_back,
    pairs,
    ppg,
    z_ref,
    start_ref,
    q_ref,
    k_ref,
    v_ref,
    out_ref,
    dout_ref,
    lse_ref,
    cos_ref,
    sin_ref,
    dqkv_ref,
    dk_acc,
    dv_acc,
):
    z = z_ref[0]
    p, b = pl.program_id(0), pl.program_id(1)
    group = p // ppg
    half = rows // 2
    offset = block_offset(z, b, n, rows)
    half_offset = pl.multiple_of(lax.rem(z - b + n, n) * half, half)
    lane = lax.broadcasted_iota(jnp.int32, (rows, LANES), 1)

    @pl.when((lax.rem(p, ppg) == 0) & (b == 0))
    def _():
        dk_acc[group] = jnp.zeros(dk_acc.shape[1:], F32)
        dv_acc[group] = jnp.zeros(dv_acc.shape[1:], F32)

    def body(back):
        width = (back + 1) * rows
        keys = window(k_ref, z, b, back, n, rows)
        values = window(v_ref, z, b, back, n, rows)
        bias = bias_of(start_ref[0], (b - back) * rows, b * rows, width, rows)
        queries = q_ref[pl.ds(offset, rows), :] * jnp.asarray(HEAD_DIM**-0.5, BF)
        outs = jnp.concatenate([out_ref[0], out_ref[1]], axis=0)
        douts = jnp.concatenate([dout_ref[0], dout_ref[1]], axis=0)
        product = outs.astype(F32) * douts.astype(F32)
        pick_row = lax.broadcasted_iota(jnp.int32, (8, LANES), 0)
        pick_lane = lax.broadcasted_iota(jnp.int32, (8, LANES), 1)
        pick = (pick_lane // HEAD_DIM == pick_row).astype(F32)
        deltas = nt(pick, product, precision=lax.Precision.HIGHEST)
        dq_parts = []
        dk_new, dv_new = None, None
        for h in range(2):
            mine = (lane >= HEAD_DIM) == (h == 1)
            q_h = jnp.where(mine, queries, jnp.zeros_like(queries))
            do_h = jnp.where(mine, douts, jnp.zeros_like(douts))
            shift = bias - lse_ref[0, 0, h : h + 1, :]
            probs = jnp.exp(nt(keys, q_h) + shift)
            d_probs = nt(values, do_h)
            d_scores = (probs * (d_probs - deltas[h : h + 1, :])).astype(BF)
            dv_h = nn(probs.astype(BF), do_h)
            dk_h = nn(d_scores, q_h)
            dv_new = dv_h if dv_new is None else dv_new + dv_h
            dk_new = dk_h if dk_new is None else dk_new + dk_h
            dq_t = tn(keys, d_scores)
            dq_parts.append(dq_t[h * HEAD_DIM : (h + 1) * HEAD_DIM])
        dq = jnp.concatenate(dq_parts, axis=0).T * HEAD_DIM**-0.5
        cos = cos_ref[pl.ds(offset, rows), :]
        sin = sin_ref[pl.ds(offset, rows), :]
        dqkv_ref[pl.ds(offset, rows), pl.ds(pl.multiple_of(p * LANES, LANES), LANES)] = rotate_slab(
            dq, cos, sin, -1.0
        ).astype(BF)
        for k in range(back + 1):
            at = pl.ds(block_offset(z, b - back + k, n, rows), rows)
            dk_acc[group, at, :] += dk_new[k * rows : (k + 1) * rows]
            dv_acc[group, at, :] += dv_new[k * rows : (k + 1) * rows]

    for back in range(max_back + 1):
        wanted = (b == back) if back < max_back else (b >= back)
        pl.when(wanted)(functools.partial(body, back))

    @pl.when((p == pairs - 1) & (b == n - 1))
    def _():
        groups = pairs // ppg
        for t in range(n):
            at = slice(t * rows, (t + 1) * rows)
            cos, sin = cos_ref[at, :], sin_ref[at, :]
            for g in range(0, groups, 2):
                slabs = []
                for acc in (dk_acc, dv_acc):
                    first = acc[g, at, :]
                    second = acc[g + 1, at, :]
                    first = first + pltpu.roll(first, HEAD_DIM, 1)
                    second = second + pltpu.roll(second, HEAD_DIM, 1)
                    slabs.append(jnp.where(lane < HEAD_DIM, first, second))
                at_k = (pairs + g // 2) * LANES
                at_v = (pairs + groups // 2 + g // 2) * LANES
                dqkv_ref[at, at_k : at_k + LANES] = rotate_slab(slabs[0], cos, sin, -1.0).astype(BF)
                dqkv_ref[at, at_v : at_v + LANES] = slabs[1].astype(BF)


def attend_back(z, starts, qkv, out, dout, lse, cos, sin, n, rows, pairs, ppg):
    total = qkv.shape[0]
    groups = pairs // ppg
    half = rows // 2
    max_back = min(n - 1, -(-(MAXLEN - 1) // rows))
    cols = (pairs + groups) * LANES
    slab = lambda p, b, z: (0, lax.rem(z[0] - b + n, n), p)
    return pl.pallas_call(
        functools.partial(attend_back_kernel, n, rows, max_back, pairs, ppg),
        out_shape=jax.ShapeDtypeStruct((total, cols), BF),
        grid_spec=pltpu.PrefetchScalarGridSpec(
            num_scalar_prefetch=1,
            grid=(pairs, n),
            in_specs=[
                pl.BlockSpec((1, 1, rows), lambda p, b, z: (b, 0, 0)),
                pl.BlockSpec((total, LANES), lambda p, b, z: (0, p)),
                pl.BlockSpec((total, LANES), lambda p, b, z: (0, pairs + p // ppg)),
                pl.BlockSpec((total, LANES), lambda p, b, z: (0, pairs + groups + p // ppg)),
                pl.BlockSpec((2, half, LANES), slab),
                pl.BlockSpec((2, half, LANES), slab),
                pl.BlockSpec((1, 1, 2, rows), lambda p, b, z: (p, b, 0, 0)),
                pl.BlockSpec((total, LANES), lambda p, b, z: (0, 0)),
                pl.BlockSpec((total, LANES), lambda p, b, z: (0, 0)),
            ],
            out_specs=pl.BlockSpec((total, cols), lambda p, b, z: (0, 0)),
            scratch_shapes=[
                pltpu.VMEM((groups, total, LANES), F32),
                pltpu.VMEM((groups, total, LANES), F32),
            ],
        ),
        cost_estimate=pl.CostEstimate(
            flops=10 * total * rows * 3 * pairs * LANES,
            bytes_accessed=8 * total * pairs * LANES,
            transcendentals=total * rows * 3 * pairs * 2,
        ),
        compiler_params=pltpu.CompilerParams(vmem_limit_bytes=VMEM_CAP),
        name="attend_back",
    )(z, starts, qkv, qkv, qkv, out, dout, lse, cos, sin)


def mlp_kernel(has_prev, x_ref, g_ref, wg_ref, wu_ref, wd_ref, *rest):
    if has_prev:
        rest = rest[2:]
    down_ref, dx_ref, gu_ref, hid_ref, down_acc, dx_acc = rest
    j = pl.program_id(0)
    tile = wg_ref.shape[1]

    @pl.when(j == 0)
    def _():
        down_acc[...] = jnp.zeros_like(down_acc)
        dx_acc[...] = jnp.zeros_like(dx_acc)

    x = x_ref[...]
    gate = nn(x, wg_ref[...])
    up = nn(x, wu_ref[...])
    d_hidden = nt(g_ref[...], wd_ref[...])
    sig = jax.nn.sigmoid(gate)
    act = gate * sig
    hidden = (act * up).astype(BF)
    d_gate = (d_hidden * up * sig * (1.0 + gate * (1.0 - sig))).astype(BF)
    d_up = (d_hidden * act).astype(BF)
    hid_ref[...] = hidden
    gu_ref[:, :tile] = d_gate
    gu_ref[:, tile:] = d_up
    down_acc[...] += nn(hidden, wd_ref[...])
    dx_acc[...] += nt(d_gate, wg_ref[...]) + nt(d_up, wu_ref[...])

    @pl.when(j == pl.num_programs(0) - 1)
    def _():
        down_ref[...] = down_acc[...].astype(BF)
        dx_ref[...] = dx_acc[...].astype(BF)


MLP_TILE = 512


def mlp_chunk(x, g, w_gate, w_up, w_down, chunk, chunks, prev):
    rows, depth = x.shape
    ff = w_gate.shape[1]
    tile = min(MLP_TILE, ff)
    in_specs = [
        pl.BlockSpec((rows, depth), lambda j: (0, 0)),
        pl.BlockSpec((rows, depth), lambda j: (0, 0)),
        pl.BlockSpec((depth, tile), lambda j: (0, j)),
        pl.BlockSpec((depth, tile), lambda j: (0, j)),
        pl.BlockSpec((tile, depth), lambda j: (j, 0)),
    ]
    args = [x, g, w_gate, w_up, w_down]
    aliases = {}
    if prev is not None:
        in_specs += [pl.BlockSpec(memory_space=pl.ANY)] * 2
        args += list(prev)
        aliases = {5: 2, 6: 3}
    return pl.pallas_call(
        functools.partial(mlp_kernel, prev is not None),
        out_shape=(
            jax.ShapeDtypeStruct((rows, depth), BF),
            jax.ShapeDtypeStruct((rows, depth), BF),
            jax.ShapeDtypeStruct((chunks * rows, 2 * ff), BF),
            jax.ShapeDtypeStruct((chunks * rows, ff), BF),
        ),
        grid=(ff // tile,),
        in_specs=in_specs,
        out_specs=(
            pl.BlockSpec((rows, depth), lambda j: (0, 0)),
            pl.BlockSpec((rows, depth), lambda j: (0, 0)),
            pl.BlockSpec((rows, 2 * tile), lambda j: (chunk, j)),
            pl.BlockSpec((rows, tile), lambda j: (chunk, j)),
        ),
        scratch_shapes=[pltpu.VMEM((rows, depth), F32), pltpu.VMEM((rows, depth), F32)],
        input_output_aliases=aliases,
        cost_estimate=pl.CostEstimate(
            flops=12 * rows * depth * ff,
            bytes_accessed=6 * depth * ff + 8 * rows * depth + 6 * rows * ff,
            transcendentals=rows * ff,
        ),
        compiler_params=pltpu.CompilerParams(vmem_limit_bytes=VMEM_CAP),
        name=f"mlp_{chunk}",
    )(*args)


def norm_rows(rows_in):
    inv = lax.rsqrt(jnp.mean(rows_in * rows_in, axis=1, keepdims=True) + epsilon)
    return rows_in * inv, inv


def norm_back(d_in, gain, normed, inv):
    scaled = d_in * gain
    return inv * (scaled - normed * jnp.mean(scaled * normed, axis=1, keepdims=True))


def make_layer(n, dp):
    def per_device(
        block_in,
        out_grad,
        segment_ids,
        w_query,
        w_key,
        w_value,
        w_out,
        w_gate,
        w_up,
        w_down,
        gain_attn,
        gain_mlp,
    ):
        seq_row = segment_ids[0]
        lr, depth = block_in.shape
        half = lr // 2
        total = seq_row.shape[0]
        z = lax.axis_index("tensor")
        z_arr = jnp.reshape(z, (1,)).astype(jnp.int32)
        pairs = w_query.shape[1] // LANES
        groups = w_key.shape[1] // HEAD_DIM
        ppg = pairs // groups
        ff = w_gate.shape[1]

        normed_one, inv_one = norm_rows(block_in)
        attn_in = (normed_one * gain_attn).astype(BF)
        attn_blocks = line_gather(attn_in, n, z)

        run_start = run_starts(seq_row)
        index_vals = jnp.arange(total, dtype=jnp.int32)
        cos, sin = rope_tables(ring_blocks(index_vals - run_start, n, z))
        starts = jnp.where(seq_row >= 0, run_start, index_vals).reshape(n, 1, lr)
        live = lax.dynamic_slice_in_dim((seq_row >= 0).astype(F32), z * lr, lr)
        masked_grad = out_grad * live[:, None]

        def doubled(w):
            heads = [w[:, g * HEAD_DIM : (g + 1) * HEAD_DIM] for g in range(groups)]
            return [part for head in heads for part in (head, head)]

        w_aug = jnp.concatenate([w_query] + doubled(w_key) + doubled(w_value), axis=1)
        w_qkv = jnp.concatenate([w_query, w_key, w_value], axis=1)

        attn_all = jnp.concatenate(attn_blocks, axis=0)
        grad_rows, attn_all = lax.optimization_barrier((masked_grad.astype(BF), attn_all))
        grad_gathered = lax.all_gather(grad_rows, "tensor", axis=0, tiled=True)

        qkv = project(attn_all, w_aug, cos, sin, pairs + groups, lr)
        attended, lse = attend(z_arr, starts, qkv, n, lr, pairs, ppg)
        out_part = nn(attended.reshape(total, -1), w_out).astype(BF)

        def pieces(array, chunk):
            base = chunk * n * half
            return [array[base + t * half : base + (t + 1) * half] for t in range(n)]

        grad_ring = []
        for chunk in range(2):
            for t in range(n):
                first = lax.rem(z - t + n, n) * lr + chunk * half
                grad_ring.append(lax.dynamic_slice_in_dim(grad_gathered, first, half))
        grad_all = jnp.concatenate(grad_ring, axis=0)

        middles, normeds, invs, mlp_ins, x_chunks = [], [], [], [], []
        for chunk in range(2):
            rows = slice(chunk * half, (chunk + 1) * half)
            middle = block_in[rows] + line_scatter(pieces(out_part, chunk), n)
            normed, inv = norm_rows(middle)
            mlp_in = (normed * gain_mlp).astype(BF)
            middles.append(middle)
            normeds.append(normed)
            invs.append(inv)
            x_chunks.append(jnp.concatenate(line_gather(mlp_in, n, z), axis=0))

        prev = None
        downs, d_mids, mid_alls = [], [], []
        for chunk in range(2):
            g_chunk = grad_all[chunk * n * half : (chunk + 1) * n * half]
            down, dx, gu, hid = mlp_chunk(
                x_chunks[chunk], g_chunk, w_gate, w_up, w_down, chunk, 2, prev
            )
            prev = (gu, hid)
            downs.append(down)
            rows = slice(chunk * half, (chunk + 1) * half)
            d_mlp = line_scatter([dx[t * half : (t + 1) * half] for t in range(n)], n)
            d_mid = masked_grad[rows] + norm_back(d_mlp, gain_mlp, normeds[chunk], invs[chunk])
            d_mids.append(d_mid)
            mid_alls.append(jnp.concatenate(line_gather(d_mid.astype(BF), n, z), axis=0))
        gu, hid = prev
        x_all = jnp.concatenate(x_chunks, axis=0)
        grad_down_t = tn(grad_all, hid).astype(BF)
        sum_down_t = lax.psum_scatter(grad_down_t, "dp", scatter_dimension=0, tiled=True)
        grad_gu = tn(x_all, gu).astype(BF)
        sum_gu = lax.psum_scatter(grad_gu, "dp", scatter_dimension=0, tiled=True)

        block_out = jnp.concatenate(
            [
                middles[c] + line_scatter([downs[c][t * half : (t + 1) * half] for t in range(n)], n)
                for c in range(2)
            ],
            axis=0,
        )

        d_attended = jnp.stack([nt(mid, w_out).astype(BF) for mid in mid_alls])
        mid_all = jnp.concatenate(mid_alls, axis=0)
        grad_out_t = tn(mid_all, attended.reshape(total, -1)).astype(BF)
        d_qkv = attend_back(
            z_arr, starts, qkv, attended, d_attended, lse, cos, sin, n, lr, pairs, ppg
        )
        d_attn_part = nt(d_qkv, w_qkv).astype(BF)
        d_attn = line_scatter([d_attn_part[t * lr : (t + 1) * lr] for t in range(n)], n)
        d_middle = jnp.concatenate(d_mids, axis=0)
        input_grad = d_middle + norm_back(d_attn, gain_attn, normed_one, inv_one)

        grad_attn = jnp.concatenate([tn(attn_all, d_qkv).astype(BF), grad_out_t], axis=1)
        sum_attn = lax.psum_scatter(grad_attn, "dp", scatter_dimension=0, tiled=True).astype(F32)

        q_cols, k_cols, v_cols = w_query.shape[1], w_key.shape[1], w_value.shape[1]
        sum_query = sum_attn[:, :q_cols]
        sum_key = sum_attn[:, q_cols : q_cols + k_cols]
        sum_value = sum_attn[:, q_cols + k_cols : q_cols + k_cols + v_cols]
        sum_out = sum_attn[:, q_cols + k_cols + v_cols :].T
        tile = min(MLP_TILE, ff)
        gu_sum = sum_gu.astype(F32).reshape(-1, ff // tile, 2, tile)
        sum_gate = gu_sum[:, :, 0].reshape(-1, ff)
        sum_up = gu_sum[:, :, 1].reshape(-1, ff)
        sum_down = sum_down_t.astype(F32).T

        mine = lax.axis_index("dp") * (depth // dp)
        my_rows = lambda w: lax.dynamic_slice_in_dim(w, mine, depth // dp).astype(F32)
        gain_attn_part = jnp.sum(my_rows(w_qkv) * sum_attn[:, : w_qkv.shape[1]], axis=1)
        gain_mlp_part = jnp.sum(my_rows(w_gate) * sum_gate + my_rows(w_up) * sum_up, axis=1)
        gains = lax.psum(jnp.stack([gain_attn_part, gain_mlp_part]), "tensor")
        total_gain_attn = gains[0] / my_rows(gain_attn)
        total_gain_mlp = gains[1] / my_rows(gain_mlp)
        return (
            block_out,
            input_grad,
            sum_query,
            sum_key,
            sum_value,
            sum_out,
            sum_gate,
            sum_up,
            sum_down,
            total_gain_attn,
            total_gain_mlp,
        )

    return per_device


def solution(mesh):
    return jax.shard_map(
        make_layer(mesh.shape["tensor"], mesh.shape["dp"]),
        mesh=mesh,
        in_specs=(
            P(("dp", "tensor"), None),
            P(("dp", "tensor"), None),
            P("dp", None),
            P(None, "tensor"),
            P(None, "tensor"),
            P(None, "tensor"),
            P("tensor", None),
            P(None, "tensor"),
            P(None, "tensor"),
            P("tensor", None),
            P(),
            P(),
        ),
        out_specs=(
            P(("dp", "tensor"), None),
            P(("dp", "tensor"), None),
            P("dp", "tensor"),
            P("dp", "tensor"),
            P("dp", "tensor"),
            P("tensor", "dp"),
            P("dp", "tensor"),
            P("dp", "tensor"),
            P("tensor", "dp"),
            P("dp"),
            P("dp"),
        ),
        check_vma=False,
    )
```
